32 devices in a mesh: row: 4 (over z), col: 8 (over y, x, core).
Axes of the slice: x: 2, y: 2, z: 4, core: 2. Of those that a mesh axis runs over, the one named last changes fastest.
Arguments:
- top_in: bfloat16 [8, 96, 1920], P('col'), may hold values from -6 to 6
- bottom_in: bfloat16 [8, 96, 1920], P('col'), may hold values from -6 to 6
- row_tensor: bfloat16 [4, 8, 20, 20, 400], P('row', 'col'), may hold values from -0.3125 to 0.3125
- left_proj: bfloat16 [2, 4, 8, 96, 1920], P(None, 'row', 'col'), may hold values from -0.125 to 0.125
- right_proj: bfloat16 [2, 4, 8, 96, 1920], P(None, 'row', 'col'), may hold values from -0.125 to 0.125
Outputs:
- env: bfloat16 [2, 4, 8, 96, 1920], P(None, 'row', 'col')
The draws below stay inside these ranges and needn't reach their ends.
All inputs are finite; a program needn't handle non-finite values.
Results may differ from the reference program's by a relative error of at most 0.014.
Values may be sent and summed in bfloat16 or wider, within the bound.
A program may use at most 128 MiB of HBM per device.

```python
import jax
import jax.numpy as jnp
from jax import lax

CHI = 96
SECTOR = 32
D2 = 20
COLS = 8
ROWS = 4


def block_scale(own_key, extent, split, least, largest):
    def one(axis_at, blocks):
        heights = jax.random.uniform(jax.random.fold_in(jax.random.fold_in(own_key, 6), axis_at), (blocks,), jnp.float32, least / len(split), largest / len(split))
        return jnp.repeat(jnp.exp(heights), extent[axis_at] // blocks).reshape((-1,) + (1,) * (len(extent) - axis_at - 1))

    factor_of = one(*split[0])
    for cut in split[1:]:
        factor_of = factor_of * one(*cut)
    return factor_of


def centred(key, shape, scale, bound, cuts=(), kind=jnp.bfloat16):
    loudness = block_scale(key, shape, cuts, -0.22, 0.18) if cuts else 1.0
    entries = jax.random.normal(key, shape, jnp.float32) * scale * loudness
    return jnp.minimum(jnp.maximum(entries, -bound), bound).astype(kind)


def setup_inputs(seed: int = 0) -> dict:
    key_of = jax.random.split(jax.random.key(seed), 6)
    return {
        "top_in": centred(key_of[0], (COLS, CHI, D2 * CHI), 1.0, 6.0, ((0, 8),)),
        "bottom_in": centred(key_of[1], (COLS, CHI, D2 * CHI), 1.0, 6.0, ((0, 8),)),
        "row_tensor": centred(key_of[2], (ROWS, COLS, D2, D2, D2 * D2), (D2 * D2) ** -0.5, 0.3125, ((0, 4), (1, 8))),
        "left_proj": centred(key_of[3], (2, ROWS, COLS, CHI, D2 * CHI), (CHI * D2) ** -0.5, 0.125, ((1, 4), (2, 8))),
        "right_proj": centred(key_of[4], (2, ROWS, COLS, CHI, D2 * CHI), (CHI * D2) ** -0.5, 0.125, ((1, 4), (2, 8))),
    }


epsilon = 1e-06

def absorb_column(boundary, row_site, left_proj, right_proj):
    blocks = CHI // SECTOR
    left_blocks = jnp.moveaxis(left_proj.reshape(CHI, D2, blocks, SECTOR), 2, 0)
    boundary_wide = boundary.astype(jnp.float32)
    site_wide = row_site.astype(jnp.float32)
    right_wide = right_proj.astype(jnp.float32)

    def one_block(block_proj):
        first_part = jnp.einsum('lLa,lur->aLur', block_proj.astype(jnp.float32), boundary_wide).astype(jnp.bfloat16)
        second_part = jnp.einsum('aLur,LuRd->Rdar', first_part.astype(jnp.float32), site_wide).astype(jnp.bfloat16)
        return jnp.einsum('Rdar,rRb->adb', second_part.astype(jnp.float32), right_wide)
    grown_site = lax.map(one_block, left_blocks).reshape(CHI, D2, CHI)
    factor = lax.rsqrt(jnp.mean(grown_site * grown_site) + epsilon)
    return (grown_site * factor).astype(jnp.bfloat16)

def absorb_row(boundary, row_sites, left_proj, right_proj):

    def one_column(items):
        return absorb_column(items[0], items[1], items[2], items[3])
    return lax.map(one_column, (boundary, row_sites, left_proj, right_proj))

def reference(top_in, bottom_in, row_tensor, left_proj, right_proj):
    down_tensor = row_tensor.reshape(ROWS, COLS, D2, D2, D2, D2)
    up_tensor = jnp.transpose(down_tensor, (0, 1, 2, 5, 4, 3))
    left_full = left_proj.reshape(2, ROWS, COLS, CHI, D2, CHI)
    right_full = right_proj.reshape(2, ROWS, COLS, CHI, D2, CHI)
    top_results = [None] * ROWS
    bottom_results = [None] * ROWS
    current = top_in.reshape(COLS, CHI, D2, CHI)
    for lattice_row in range(ROWS):
        current = absorb_row(current, down_tensor[lattice_row], jnp.roll(left_full[0, lattice_row], 1, axis=0), right_full[0, lattice_row])
        top_results[lattice_row] = current
    current = bottom_in.reshape(COLS, CHI, D2, CHI)
    for lattice_row in range(ROWS - 1, -1, -1):
        current = absorb_row(current, up_tensor[lattice_row], jnp.roll(left_full[1, lattice_row], 1, axis=0), right_full[1, lattice_row])
        bottom_results[lattice_row] = current
    stacked = jnp.stack([jnp.stack(top_results), jnp.stack(bottom_results)])
    return stacked.reshape(2, ROWS, COLS, CHI, D2 * CHI)
```

```python
import functools

import jax
import jax.numpy as jnp
from jax import lax
from jax.experimental import pallas as pl
from jax.experimental.pallas import tpu as pltpu
from jax.sharding import PartitionSpec as P

epsilon = 1e-06
LANES = 128
CHUNK = 16


def round_up(value, unit):
    return -(-value // unit) * unit


def absorb_kernel(chi, pair, padded, chunk, role, held_ref, left_ref, site_ref, right_ref, out_ref,
                  wide, right_wide, first, spread, turned, grown, total):
    step = pl.program_id(0)
    active = role[0] == 1

    @pl.when(active & (step == 0))
    def _():
        total[...] = jnp.zeros_like(total)
        wide[...] = jnp.zeros_like(wide)
        right_wide[...] = jnp.zeros_like(right_wide)
        for leg in range(pair):
            wide[:, leg * LANES:leg * LANES + chi] = held_ref[:, leg * chi:(leg + 1) * chi]
            right_wide[leg * LANES:leg * LANES + chi, :chi] = right_ref[0, :, leg * chi:(leg + 1) * chi]

    @pl.when(active)
    def _():
        for duo in range(pair // 2):
            part = jnp.dot(
                left_ref[0], wide[:, duo * 2 * LANES:(duo + 1) * 2 * LANES],
                preferred_element_type=jnp.float32,
            )
            for bond in range(chunk):
                rows = part[bond * padded:(bond + 1) * padded]
                both = jnp.concatenate([rows[:, :LANES], rows[:, LANES:]], axis=0)
                first[duo * 2 * padded:(duo + 1) * 2 * padded, bond * LANES:(bond + 1) * LANES] = both.astype(jnp.bfloat16)
        for duo in range(chunk // 2):
            second = jnp.dot(
                site_ref[0], first[:, duo * 2 * LANES:(duo + 1) * 2 * LANES],
                preferred_element_type=jnp.float32,
            )
            for leg in range(pair):
                rows = second[leg * padded:(leg + 1) * padded]
                both = jnp.concatenate([rows[:, :LANES], rows[:, LANES:]], axis=0)
                spread[duo * 2 * padded:(duo + 1) * 2 * padded, leg * LANES:(leg + 1) * LANES] = both.astype(jnp.bfloat16)
        done = jnp.dot(spread[...], right_wide[...], preferred_element_type=jnp.float32)
        total[...] += jnp.sum((done * done).reshape(-1, 8, LANES), axis=0)
        turned[...] = done
        at = pl.multiple_of(step * chunk, chunk)
        for leg in range(pair):
            rows = turned[pl.ds(leg, chunk, stride=padded), :]
            grown[pl.ds(at, chunk), leg * chi:(leg + 1) * chi] = rows[:, :chi]

    @pl.when(active & (step == pl.num_programs(0) - 1))
    def _():
        mean = jnp.sum(total[...]) / (chi * pair * chi)
        factor = lax.rsqrt(jnp.full((1, 1), mean + epsilon, jnp.float32))
        out_ref[...] = (grown[...] * factor).astype(jnp.bfloat16)


def absorb(role, held, left, site, right, chi, pair, padded):
    chunk = CHUNK
    return pl.pallas_call(
        functools.partial(absorb_kernel, chi, pair, padded, chunk),
        out_shape=jax.ShapeDtypeStruct(held.shape, held.dtype),
        grid_spec=pltpu.PrefetchScalarGridSpec(
            num_scalar_prefetch=1,
            grid=(chi // chunk,),
            in_specs=[
                pl.BlockSpec(held.shape, lambda s, role: (0, 0)),
                pl.BlockSpec((1, chunk * padded, chi), lambda s, role: (role[1], s, 0)),
                pl.BlockSpec((1,) + site.shape[1:], lambda s, role: (role[1], 0, 0)),
                pl.BlockSpec((1,) + right.shape[1:], lambda s, role: (role[1], 0, 0)),
            ],
            out_specs=pl.BlockSpec(held.shape, lambda s, role: (0, 0)),
            scratch_shapes=[
                pltpu.VMEM((chi, pair * LANES), jnp.bfloat16),
                pltpu.VMEM((pair * LANES, LANES), jnp.bfloat16),
                pltpu.VMEM((pair * padded, chunk * LANES), jnp.bfloat16),
                pltpu.VMEM((chunk * padded, pair * LANES), jnp.bfloat16),
                pltpu.VMEM((chunk * padded, LANES), jnp.float32),
                pltpu.VMEM(held.shape, jnp.float32),
                pltpu.VMEM((8, LANES), jnp.float32),
            ],
        ),
        name="absorb",
    )(role, held, left, site, right)


def local(top_in, bottom_in, row_tensor, left_proj, right_proj):
    row_count = lax.axis_size("row")
    col_count = lax.axis_size("col")
    row_index = lax.axis_index("row")
    chi = top_in.shape[1]
    pair = row_tensor.shape[2]
    padded = round_up(pair, 8)
    extra = padded - pair

    ring = [(source, (source + 1) % col_count) for source in range(col_count)]
    incoming = lax.ppermute(left_proj[:, 0, 0], "col", ring)
    left = jnp.transpose(incoming.reshape(2, chi, pair, chi), (0, 3, 2, 1))
    left = jnp.pad(left, ((0, 0), (0, 0), (0, extra), (0, 0))).reshape(2, chi * padded, chi)
    right = right_proj[:, 0, 0]
    tensor = row_tensor[0, 0].reshape(pair, pair, pair, pair)
    sites = jnp.stack([jnp.transpose(tensor, (2, 3, 1, 0)), jnp.transpose(tensor, (2, 1, 3, 0))])
    sites = jnp.pad(sites, ((0, 0), (0, 0), (0, extra), (0, 0), (0, extra)))
    sites = sites.reshape(2, pair * padded, pair * padded)

    held = jnp.where(row_index < row_count // 2, top_in[0], bottom_in[0])
    top_env = bottom_env = None
    for turn in range(row_count):
        top_turn = row_index == turn
        bottom_turn = row_index == row_count - 1 - turn
        role = jnp.stack([top_turn | bottom_turn, bottom_turn]).astype(jnp.int32)
        result = absorb(role, held, left, sites, right, chi, pair, padded)
        top_env = result if turn == 0 else jnp.where(top_turn, result, top_env)
        bottom_env = result if turn == 0 else jnp.where(bottom_turn, result, bottom_env)
        if turn + 1 < row_count:
            held = lax.ppermute(
                result, "row",
                [(turn, turn + 1), (row_count - 1 - turn, row_count - 2 - turn)],
            )
    return jnp.stack([top_env, bottom_env])[:, None, None]


def solution(mesh):
    return jax.shard_map(
        local,
        mesh=mesh,
        in_specs=(
            P("col", None, None),
            P("col", None, None),
            P("row", "col", None, None, None),
            P(None, "row", "col", None, None),
            P(None, "row", "col", None, None),
        ),
        out_specs=P(None, "row", "col", None, None),
        check_vma=False,
    )
```

```python
import functools

import jax
import jax.numpy as jnp
from jax import lax
from jax.experimental import pallas as pl
from jax.experimental.pallas import tpu as pltpu
from jax.sharding import PartitionSpec as P

epsilon = 1e-06
LANES = 128
CHUNK = 16


def round_up(value, unit):
    return -(-value // unit) * unit


def sweep_kernel(rows, chi, pair, padded, chunk, held_ref, left_ref, site_ref, right_ref, env_ref,
                 wide, left_tall, left_rows, right_wide, first, spread, turned, grown, total, stage, landed, scaling, send_sem, recv_sem):
    row = lax.axis_index("row")
    blocks = chi // chunk
    begin = jnp.where(row < rows // 2, 0, 1)

    barrier = pltpu.get_barrier_semaphore()

    @pl.when(row > 0)
    def _():
        pl.semaphore_signal(barrier, inc=1, device_id={"row": row - 1}, device_id_type=pl.DeviceIdType.MESH)

    @pl.when(row < rows - 1)
    def _():
        pl.semaphore_signal(barrier, inc=1, device_id={"row": row + 1}, device_id_type=pl.DeviceIdType.MESH)

    pl.semaphore_wait(barrier, jnp.where(row > 0, 1, 0) + jnp.where(row < rows - 1, 1, 0))

    wide[...] = jnp.zeros_like(wide)
    right_wide[...] = jnp.zeros_like(right_wide)
    left_tall[...] = jnp.zeros_like(left_tall)

    def prepare(which):
        for leg in range(pair):
            right_wide[which, leg * LANES:leg * LANES + chi, :chi] = right_ref[which, :, leg * chi:(leg + 1) * chi]
            piece = left_ref[which, :, leg * chi:(leg + 1) * chi].astype(jnp.float32)
            left_tall[pl.ds(leg, chi, stride=padded), :chi] = piece.T
        left_rows[which] = left_tall[...].astype(jnp.bfloat16)

    def copy_of(which, block):
        at = pl.multiple_of(block * chunk, chunk)
        return pltpu.make_async_remote_copy(
            src_ref=stage.at[which, pl.ds(at, chunk)],
            dst_ref=landed.at[which, pl.ds(at, chunk)],
            send_sem=send_sem.at[which, block],
            recv_sem=recv_sem.at[which, block],
            device_id={"row": jnp.where(which == 0, row + 1, row - 1)},
            device_id_type=pl.DeviceIdType.MESH,
        )

    def inverse_norm(square_sum):
        return lax.rsqrt(jnp.full((1, 1), jnp.sum(square_sum) / (chi * pair * chi) + epsilon, jnp.float32))

    def absorb(which, sends):
        total[...] = jnp.zeros_like(total)

        def one_block(block, carry):
            at = pl.multiple_of(block * chunk, chunk)
            left_here = left_rows[which, pl.ds(pl.multiple_of(block * chunk * padded, chunk * padded), chunk * padded), :]
            for duo in range(pair // 2):
                part = jnp.dot(
                    left_here, wide[:, duo * 2 * LANES:(duo + 1) * 2 * LANES],
                    preferred_element_type=jnp.float32,
                )
                for bond in range(chunk):
                    piece = part[bond * padded:(bond + 1) * padded]
                    both = jnp.concatenate([piece[:, :LANES], piece[:, LANES:]], axis=0)
                    first[duo * 2 * padded:(duo + 1) * 2 * padded, bond * LANES:(bond + 1) * LANES] = both.astype(jnp.bfloat16)
            for duo in range(chunk // 2):
                second = jnp.dot(
                    site_ref[which], first[:, duo * 2 * LANES:(duo + 1) * 2 * LANES],
                    preferred_element_type=jnp.float32,
                )
                for leg in range(pair):
                    piece = second[leg * padded:(leg + 1) * padded]
                    both = jnp.concatenate([piece[:, :LANES], piece[:, LANES:]], axis=0)
                    spread[duo * 2 * padded:(duo + 1) * 2 * padded, leg * LANES:(leg + 1) * LANES] = both.astype(jnp.bfloat16)
            done = jnp.dot(spread[...], right_wide[which], preferred_element_type=jnp.float32) * scaling[...]
            total[...] += jnp.sum((done * done).reshape(-1, 8, LANES), axis=0)
            turned[...] = done
            for leg in range(pair):
                piece = turned[pl.ds(leg, chunk, stride=padded), :]
                grown[pl.ds(at, chunk), leg * chi:(leg + 1) * chi] = piece[:, :chi]
            stage[which, pl.ds(at, chunk), :] = grown[pl.ds(at, chunk), :].astype(jnp.bfloat16)

            @pl.when(sends & (block > 0))
            def _():
                copy_of(which, block - 1).start()

            return carry

        lax.fori_loop(0, blocks, one_block, 0)
        factor = inverse_norm(total[...])
        env_ref[which] = (grown[...] * factor).astype(jnp.bfloat16)

        @pl.when(sends)
        def _():
            copy_of(which, blocks - 1).start()

    def unpack(source):
        for leg in range(pair):
            wide[:chi, leg * LANES:leg * LANES + chi] = source[:, leg * chi:(leg + 1) * chi]

    def one_turn(turn, carry):
        which = jnp.where(row == turn, 0, 1)
        active = (row == turn) | (row == rows - 1 - turn)
        sends = turn < rows - 1

        @pl.when(turn == 0)
        def _():
            prepare(begin)

        @pl.when(active & (turn == 0))
        def _():
            unpack(held_ref[...])
            scaling[...] = jnp.ones_like(scaling)

        @pl.when(active & (turn > 0))
        def _():
            for block in range(blocks):
                copy_of(which, block).wait_recv()
            unpack(landed[which])
            values = landed[which].astype(jnp.float32)
            scaling[...] = jnp.broadcast_to(inverse_norm(values * values), scaling.shape)

        @pl.when(active)
        def _():
            absorb(which, sends)

        @pl.when(turn == 0)
        def _():
            prepare(1 - begin)

        @pl.when(active & sends)
        def _():
            for block in range(blocks):
                copy_of(which, block).wait_send()

        return carry

    lax.fori_loop(0, rows, one_turn, 0)


def sweep(rows, held, left, site, right, chi, pair, padded):
    chunk = CHUNK
    blocks = chi // chunk
    return pl.pallas_call(
        functools.partial(sweep_kernel, rows, chi, pair, padded, chunk),
        out_shape=jax.ShapeDtypeStruct((2,) + held.shape, held.dtype),
        in_specs=[pl.BlockSpec(memory_space=pltpu.VMEM)] * 4,
        out_specs=pl.BlockSpec(memory_space=pltpu.VMEM),
        scratch_shapes=[
            pltpu.VMEM((LANES, pair * LANES), jnp.bfloat16),
            pltpu.VMEM((chi * padded, LANES), jnp.float32),
            pltpu.VMEM((2, chi * padded, LANES), jnp.bfloat16),
            pltpu.VMEM((2, pair * LANES, LANES), jnp.bfloat16),
            pltpu.VMEM((pair * padded, chunk * LANES), jnp.bfloat16),
            pltpu.VMEM((chunk * padded, pair * LANES), jnp.bfloat16),
            pltpu.VMEM((chunk * padded, LANES), jnp.float32),
            pltpu.VMEM(held.shape, jnp.float32),
            pltpu.VMEM((8, LANES), jnp.float32),
            pltpu.VMEM((2,) + held.shape, jnp.bfloat16),
            pltpu.VMEM((2,) + held.shape, jnp.bfloat16),
            pltpu.VMEM((1, LANES), jnp.float32),
            pltpu.SemaphoreType.DMA((2, blocks)),
            pltpu.SemaphoreType.DMA((2, blocks)),
        ],
        compiler_params=pltpu.CompilerParams(collective_id=0, has_side_effects=True, vmem_limit_bytes=56 * 1024 * 1024),
        name="sweep",
    )(held, left, site, right)


def local(top_in, bottom_in, row_tensor, left_proj, right_proj):
    row_count = lax.axis_size("row")
    col_count = lax.axis_size("col")
    row_index = lax.axis_index("row")
    chi = top_in.shape[1]
    pair = row_tensor.shape[2]
    padded = round_up(pair, 8)
    extra = padded - pair

    ring = [(source, (source + 1) % col_count) for source in range(col_count)]
    left = lax.ppermute(left_proj[:, 0, 0], "col", ring)
    right = right_proj[:, 0, 0]
    tensor = row_tensor[0, 0].reshape(pair, pair, pair, pair)
    sites = jnp.stack([jnp.transpose(tensor, (2, 3, 1, 0)), jnp.transpose(tensor, (2, 1, 3, 0))])
    sites = jnp.pad(sites, ((0, 0), (0, 0), (0, extra), (0, 0), (0, extra)))
    sites = sites.reshape(2, pair * padded, pair * padded)

    held = jnp.where(row_index < row_count // 2, top_in[0], bottom_in[0])
    env = sweep(row_count, held, left, sites, right, chi, pair, padded)
    return env[:, None, None]


def solution(mesh):
    return jax.shard_map(
        local,
        mesh=mesh,
        in_specs=(
            P("col", None, None),
            P("col", None, None),
            P("row", "col", None, None, None),
            P(None, "row", "col", None, None),
            P(None, "row", "col", None, None),
        ),
        out_specs=P(None, "row", "col", None, None),
        check_vma=False,
    )
```

```python
import functools

import jax
import jax.numpy as jnp
from jax import lax
from jax.experimental import pallas as pl
from jax.experimental.pallas import tpu as pltpu
from jax.sharding import PartitionSpec as P

epsilon = 1e-06
LANES = 128
CHUNK = 16


def round_up(value, unit):
    return -(-value // unit) * unit


def sweep_kernel(rows, chi, pair, padded, chunk, held_ref, left_ref, site_ref, right_ref, env_ref,
                 wide, left_tall, left_rows, right_wide, first, spread, turned, grown, total, stage, landed, scaling, send_sem, recv_sem):
    row = lax.axis_index("row")
    blocks = chi // chunk
    begin = jnp.where(row < rows // 2, 0, 1)

    barrier = pltpu.get_barrier_semaphore()

    @pl.when(row > 0)
    def _():
        pl.semaphore_signal(barrier, inc=1, device_id={"row": row - 1}, device_id_type=pl.DeviceIdType.MESH)

    @pl.when(row < rows - 1)
    def _():
        pl.semaphore_signal(barrier, inc=1, device_id={"row": row + 1}, device_id_type=pl.DeviceIdType.MESH)

    pl.semaphore_wait(barrier, jnp.where(row > 0, 1, 0) + jnp.where(row < rows - 1, 1, 0))

    wide[...] = jnp.zeros_like(wide)
    right_wide[...] = jnp.zeros_like(right_wide)
    left_tall[...] = jnp.zeros_like(left_tall)

    def prepare(which):
        for leg in range(pair):
            right_wide[which, leg * LANES:leg * LANES + chi, :chi] = right_ref[which, :, leg * chi:(leg + 1) * chi]
            piece = left_ref[which, :, leg * chi:(leg + 1) * chi].astype(jnp.float32)
            left_tall[pl.ds(leg, chi, stride=padded), :chi] = piece.T
        left_rows[which] = left_tall[...].astype(jnp.bfloat16)

    def copy_of(which, block):
        at = pl.multiple_of(block * chunk, chunk)
        return pltpu.make_async_remote_copy(
            src_ref=stage.at[which, pl.ds(at, chunk)],
            dst_ref=landed.at[which, pl.ds(at, chunk)],
            send_sem=send_sem.at[which, block],
            recv_sem=recv_sem.at[which, block],
            device_id={"row": jnp.where(which == 0, row + 1, row - 1)},
            device_id_type=pl.DeviceIdType.MESH,
        )

    def inverse_norm(square_sum):
        return lax.rsqrt(jnp.full((1, 1), jnp.sum(square_sum) / (chi * pair * chi) + epsilon, jnp.float32))

    def absorb(which, sends):
        total[...] = jnp.zeros_like(total)

        def one_block(block, carry):
            at = pl.multiple_of(block * chunk, chunk)
            left_here = left_rows[which, pl.ds(pl.multiple_of(block * chunk * padded, chunk * padded), chunk * padded), :]
            for duo in range(pair // 2):
                part = jnp.dot(
                    left_here, wide[:, duo * 2 * LANES:(duo + 1) * 2 * LANES],
                    preferred_element_type=jnp.float32,
                )
                for bond in range(chunk):
                    piece = part[bond * padded:(bond + 1) * padded]
                    both = jnp.concatenate([piece[:, :LANES], piece[:, LANES:]], axis=0)
                    first[duo * 2 * padded:(duo + 1) * 2 * padded, bond * LANES:(bond + 1) * LANES] = both.astype(jnp.bfloat16)
            for duo in range(chunk // 2):
                second = jnp.dot(
                    site_ref[which], first[:, duo * 2 * LANES:(duo + 1) * 2 * LANES],
                    preferred_element_type=jnp.float32,
                )
                for leg in range(pair):
                    piece = second[leg * padded:(leg + 1) * padded]
                    both = jnp.concatenate([piece[:, :LANES], piece[:, LANES:]], axis=0)
                    spread[duo * 2 * padded:(duo + 1) * 2 * padded, leg * LANES:(leg + 1) * LANES] = both.astype(jnp.bfloat16)
            done = jnp.dot(spread[...], right_wide[which], preferred_element_type=jnp.float32) * scaling[...]
            total[...] += jnp.sum((done * done).reshape(-1, 8, LANES), axis=0)
            turned[...] = done
            for leg in range(pair):
                piece = turned[pl.ds(leg, chunk, stride=padded), :]
                grown[pl.ds(at, chunk), leg * chi:(leg + 1) * chi] = piece[:, :chi]
            stage[which, pl.ds(at, chunk), :] = grown[pl.ds(at, chunk), :].astype(jnp.bfloat16)

            @pl.when(sends & (block > 0))
            def _():
                copy_of(which, block - 1).start()

            return carry

        lax.fori_loop(0, blocks, one_block, 0)
        factor = inverse_norm(total[...])
        env_ref[which] = (grown[...] * factor).astype(jnp.bfloat16)

        @pl.when(sends)
        def _():
            copy_of(which, blocks - 1).start()

    def unpack(source):
        for leg in range(pair):
            wide[:chi, leg * LANES:leg * LANES + chi] = source[:, leg * chi:(leg + 1) * chi]

    def one_turn(turn, carry):
        which = jnp.where(row == turn, 0, 1)
        active = (row == turn) | (row == rows - 1 - turn)
        sends = turn < rows - 1

        @pl.when(turn == 0)
        def _():
            prepare(begin)

        @pl.when(active & (turn == 0))
        def _():
            unpack(held_ref[...])
            scaling[...] = jnp.ones_like(scaling)

        @pl.when(active & (turn > 0))
        def _():
            for block in range(blocks):
                copy_of(which, block).wait_recv()
            unpack(landed[which])
            values = landed[which].astype(jnp.float32)
            scaling[...] = jnp.broadcast_to(inverse_norm(values * values), scaling.shape)

        @pl.when(active)
        def _():
            absorb(which, sends)

        @pl.when(turn == 0)
        def _():
            prepare(1 - begin)

        @pl.when(active & sends)
        def _():
            for block in range(blocks):
                copy_of(which, block).wait_send()

        return carry

    lax.fori_loop(0, rows, one_turn, 0)


def arrange_kernel(pair, padded, tensor_ref, site_ref, tall, turned, pieces):
    width = pair * padded
    slabs = tall.shape[0]
    tall[...] = jnp.zeros_like(tall)
    pieces[...] = jnp.zeros_like(pieces)
    for leg in range(pair):
        plane = tensor_ref[leg].astype(jnp.float32)
        for slab in range(slabs):
            part = plane[:, slab * LANES:(slab + 1) * LANES]
            part = jnp.pad(part, ((0, 0), (0, LANES - part.shape[1])))
            tall[slab, pl.ds(leg, pair, stride=padded), :] = part
    for slab in range(slabs):
        for other in range(slabs):
            block = tall[slab, other * LANES:(other + 1) * LANES, :]
            turned[other, slab * LANES:(slab + 1) * LANES, :] = block.T
    gap = jnp.zeros((padded - pair, LANES), jnp.float32)
    for slab in range(slabs):
        lanes = min(LANES, width - slab * LANES)
        for duo in range(pair // 2):
            at = duo * 2 * pair
            rows = jnp.concatenate(
                [turned[slab, at:at + pair, :], gap, turned[slab, at + pair:at + 2 * pair, :], gap], axis=0
            )
            site_ref[0, duo * 2 * padded:(duo + 1) * 2 * padded, slab * LANES:slab * LANES + lanes] = (
                rows[:, :lanes].astype(jnp.bfloat16)
            )
    for low in range(pair):
        rows = jnp.concatenate(
            [turned[slab, pl.ds(low, pair, stride=pair), :] for slab in range(slabs)], axis=1
        )
        for high in range(pair):
            pieces[high, :pair, low * padded:(low + 1) * padded] = rows[:, high * padded:(high + 1) * padded]
    tall[...] = jnp.zeros_like(tall)
    for slab in range(slabs):
        lanes = min(LANES, width - slab * LANES)
        for high in range(pair):
            tall[slab, pl.ds(high, pair, stride=padded), :] = pieces[high, :pair, slab * LANES:(slab + 1) * LANES]
        site_ref[1, :, slab * LANES:slab * LANES + lanes] = tall[slab, :width, :lanes].astype(jnp.bfloat16)


def arrange(tensor, pair, padded):
    width = pair * padded
    slabs = round_up(width, LANES) // LANES
    return pl.pallas_call(
        functools.partial(arrange_kernel, pair, padded),
        out_shape=jax.ShapeDtypeStruct((2, width, width), tensor.dtype),
        scratch_shapes=[
            pltpu.VMEM((slabs, slabs * LANES, LANES), jnp.float32),
            pltpu.VMEM((slabs, slabs * LANES, LANES), jnp.float32),
            pltpu.VMEM((pair, padded, slabs * LANES), jnp.float32),
        ],
        name="arrange",
    )(tensor)


def sweep(rows, held, left, site, right, chi, pair, padded):
    chunk = CHUNK
    blocks = chi // chunk
    return pl.pallas_call(
        functools.partial(sweep_kernel, rows, chi, pair, padded, chunk),
        out_shape=jax.ShapeDtypeStruct((2,) + held.shape, held.dtype),
        in_specs=[pl.BlockSpec(memory_space=pltpu.VMEM)] * 4,
        out_specs=pl.BlockSpec(memory_space=pltpu.VMEM),
        scratch_shapes=[
            pltpu.VMEM((LANES, pair * LANES), jnp.bfloat16),
            pltpu.VMEM((chi * padded, LANES), jnp.float32),
            pltpu.VMEM((2, chi * padded, LANES), jnp.bfloat16),
            pltpu.VMEM((2, pair * LANES, LANES), jnp.bfloat16),
            pltpu.VMEM((pair * padded, chunk * LANES), jnp.bfloat16),
            pltpu.VMEM((chunk * padded, pair * LANES), jnp.bfloat16),
            pltpu.VMEM((chunk * padded, LANES), jnp.float32),
            pltpu.VMEM(held.shape, jnp.float32),
            pltpu.VMEM((8, LANES), jnp.float32),
            pltpu.VMEM((2,) + held.shape, jnp.bfloat16),
            pltpu.VMEM((2,) + held.shape, jnp.bfloat16),
            pltpu.VMEM((1, LANES), jnp.float32),
            pltpu.SemaphoreType.DMA((2, blocks)),
            pltpu.SemaphoreType.DMA((2, blocks)),
        ],
        compiler_params=pltpu.CompilerParams(collective_id=0, has_side_effects=True, vmem_limit_bytes=56 * 1024 * 1024),
        name="sweep",
    )(held, left, site, right)


def local(top_in, bottom_in, row_tensor, left_proj, right_proj):
    row_count = lax.axis_size("row")
    col_count = lax.axis_size("col")
    row_index = lax.axis_index("row")
    chi = top_in.shape[1]
    pair = row_tensor.shape[2]
    padded = round_up(pair, 8)

    ring = [(source, (source + 1) % col_count) for source in range(col_count)]
    left = lax.ppermute(left_proj[:, 0, 0], "col", ring)
    right = right_proj[:, 0, 0]
    sites = arrange(row_tensor[0, 0], pair, padded)

    held = jnp.where(row_index < row_count // 2, top_in[0], bottom_in[0])
    env = sweep(row_count, held, left, sites, right, chi, pair, padded)
    return env[:, None, None]


def solution(mesh):
    return jax.shard_map(
        local,
        mesh=mesh,
        in_specs=(
            P("col", None, None),
            P("col", None, None),
            P("row", "col", None, None, None),
            P(None, "row", "col", None, None),
            P(None, "row", "col", None, None),
        ),
        out_specs=P(None, "row", "col", None, None),
        check_vma=False,
    )
```

```python
import functools

import jax
import jax.numpy as jnp
from jax import lax
from jax.experimental import pallas as pl
from jax.experimental.pallas import tpu as pltpu
from jax.sharding import PartitionSpec as P

epsilon = 1e-06
LANES = 128
CHUNK = 16


def round_up(value, unit):
    return -(-value // unit) * unit


def sweep_kernel(rows, chi, pair, padded, chunk, held_ref, left_ref, site_ref, right_ref, env_ref,
                 wide, left_tall, left_rows, right_wide, first, spread, turned, grown, total, stage, landed, scaling, send_sem, recv_sem):
    row = lax.axis_index("row")
    blocks = chi // chunk
    begin = jnp.where(row < rows // 2, 0, 1)

    barrier = pltpu.get_barrier_semaphore()

    @pl.when(row > 0)
    def _():
        pl.semaphore_signal(barrier, inc=1, device_id={"row": row - 1}, device_id_type=pl.DeviceIdType.MESH)

    @pl.when(row < rows - 1)
    def _():
        pl.semaphore_signal(barrier, inc=1, device_id={"row": row + 1}, device_id_type=pl.DeviceIdType.MESH)

    pl.semaphore_wait(barrier, jnp.where(row > 0, 1, 0) + jnp.where(row < rows - 1, 1, 0))

    wide[...] = jnp.zeros_like(wide)
    right_wide[...] = jnp.zeros_like(right_wide)
    left_tall[...] = jnp.zeros_like(left_tall)

    def prepare(which):
        for leg in range(pair):
            right_wide[which, leg * LANES:leg * LANES + chi, :chi] = right_ref[which, :, leg * chi:(leg + 1) * chi]
            piece = left_ref[which, :, leg * chi:(leg + 1) * chi].astype(jnp.float32)
            left_tall[pl.ds(leg, chi, stride=padded), :chi] = piece.T
        left_rows[which] = left_tall[...].astype(jnp.bfloat16)

    def copy_of(which, block):
        at = pl.multiple_of(block * chunk, chunk)
        return pltpu.make_async_remote_copy(
            src_ref=stage.at[which, pl.ds(at, chunk)],
            dst_ref=landed.at[which, pl.ds(at, chunk)],
            send_sem=send_sem.at[which, block],
            recv_sem=recv_sem.at[which, block],
            device_id={"row": jnp.where(which == 0, row + 1, row - 1)},
            device_id_type=pl.DeviceIdType.MESH,
        )

    def inverse_norm(square_sum):
        return lax.rsqrt(jnp.full((1, 1), jnp.sum(square_sum) / (chi * pair * chi) + epsilon, jnp.float32))

    def absorb(which, sends):
        total[...] = jnp.zeros_like(total)

        def one_block(block, carry):
            at = pl.multiple_of(block * chunk, chunk)
            left_here = left_rows[which, pl.ds(pl.multiple_of(block * chunk * padded, chunk * padded), chunk * padded), :]
            for duo in range(pair // 2):
                part = jnp.dot(
                    left_here, wide[:, duo * 2 * LANES:(duo + 1) * 2 * LANES],
                    preferred_element_type=jnp.float32,
                )
                for bond in range(chunk):
                    piece = part[bond * padded:(bond + 1) * padded]
                    both = jnp.concatenate([piece[:, :LANES], piece[:, LANES:]], axis=0)
                    first[duo * 2 * padded:(duo + 1) * 2 * padded, bond * LANES:(bond + 1) * LANES] = both.astype(jnp.bfloat16)
            for quad in range(chunk // 4):
                second = jnp.dot(
                    site_ref[which], first[:, quad * 4 * LANES:(quad + 1) * 4 * LANES],
                    preferred_element_type=jnp.float32,
                )
                for half in range(2):
                    duo = quad * 2 + half
                    for leg in range(pair):
                        piece = second[leg * padded:(leg + 1) * padded, half * 2 * LANES:(half + 1) * 2 * LANES]
                        both = jnp.concatenate([piece[:, :LANES], piece[:, LANES:]], axis=0)
                        spread[duo * 2 * padded:(duo + 1) * 2 * padded, leg * LANES:(leg + 1) * LANES] = both.astype(jnp.bfloat16)
            middle = pair // 2 * LANES
            halves = [
                jnp.dot(spread[:, :middle], right_wide[which, :middle], preferred_element_type=jnp.float32),
                jnp.dot(spread[:, middle:], right_wide[which, middle:], preferred_element_type=jnp.float32),
            ]
            done = (halves[0] + halves[1]) * scaling[...]
            total[...] += jnp.sum((done * done).reshape(-1, 8, LANES), axis=0)
            turned[...] = done
            for leg in range(pair):
                piece = turned[pl.ds(leg, chunk, stride=padded), :]
                grown[pl.ds(at, chunk), leg * chi:(leg + 1) * chi] = piece[:, :chi]
            stage[which, pl.ds(at, chunk), :] = grown[pl.ds(at, chunk), :].astype(jnp.bfloat16)

            @pl.when(sends & (block > 0))
            def _():
                copy_of(which, block - 1).start()

            return carry

        lax.fori_loop(0, blocks, one_block, 0)
        factor = inverse_norm(total[...])
        env_ref[which] = (grown[...] * factor).astype(jnp.bfloat16)

        @pl.when(sends)
        def _():
            copy_of(which, blocks - 1).start()

    def unpack(source):
        for leg in range(pair):
            wide[:chi, leg * LANES:leg * LANES + chi] = source[:, leg * chi:(leg + 1) * chi]

    def one_turn(turn, carry):
        which = jnp.where(row == turn, 0, 1)
        active = (row == turn) | (row == rows - 1 - turn)
        sends = turn < rows - 1

        @pl.when(turn == 0)
        def _():
            prepare(begin)

        @pl.when(active & (turn == 0))
        def _():
            unpack(held_ref[...])
            scaling[...] = jnp.ones_like(scaling)

        @pl.when(active & (turn > 0))
        def _():
            for block in range(blocks):
                copy_of(which, block).wait_recv()
            unpack(landed[which])
            values = landed[which].astype(jnp.float32)
            scaling[...] = jnp.broadcast_to(inverse_norm(values * values), scaling.shape)

        @pl.when(active)
        def _():
            absorb(which, sends)

        @pl.when(turn == 0)
        def _():
            prepare(1 - begin)

        @pl.when(active & sends)
        def _():
            for block in range(blocks):
                copy_of(which, block).wait_send()

        return carry

    lax.fori_loop(0, rows, one_turn, 0)


def arrange_kernel(pair, padded, tensor_ref, site_ref, tall, turned, pieces):
    width = pair * padded
    slabs = tall.shape[0]
    tall[...] = jnp.zeros_like(tall)
    pieces[...] = jnp.zeros_like(pieces)
    for leg in range(pair):
        plane = tensor_ref[leg].astype(jnp.float32)
        for slab in range(slabs):
            part = plane[:, slab * LANES:(slab + 1) * LANES]
            part = jnp.pad(part, ((0, 0), (0, LANES - part.shape[1])))
            tall[slab, pl.ds(leg, pair, stride=padded), :] = part
    for slab in range(slabs):
        for other in range(slabs):
            block = tall[slab, other * LANES:(other + 1) * LANES, :]
            turned[other, slab * LANES:(slab + 1) * LANES, :] = block.T
    gap = jnp.zeros((padded - pair, LANES), jnp.float32)
    for slab in range(slabs):
        lanes = min(LANES, width - slab * LANES)
        for duo in range(pair // 2):
            at = duo * 2 * pair
            rows = jnp.concatenate(
                [turned[slab, at:at + pair, :], gap, turned[slab, at + pair:at + 2 * pair, :], gap], axis=0
            )
            site_ref[0, duo * 2 * padded:(duo + 1) * 2 * padded, slab * LANES:slab * LANES + lanes] = (
                rows[:, :lanes].astype(jnp.bfloat16)
            )
    for low in range(pair):
        rows = jnp.concatenate(
            [turned[slab, pl.ds(low, pair, stride=pair), :] for slab in range(slabs)], axis=1
        )
        for high in range(pair):
            pieces[high, :pair, low * padded:(low + 1) * padded] = rows[:, high * padded:(high + 1) * padded]
    tall[...] = jnp.zeros_like(tall)
    for slab in range(slabs):
        lanes = min(LANES, width - slab * LANES)
        for high in range(pair):
            tall[slab, pl.ds(high, pair, stride=padded), :] = pieces[high, :pair, slab * LANES:(slab + 1) * LANES]
        site_ref[1, :, slab * LANES:slab * LANES + lanes] = tall[slab, :width, :lanes].astype(jnp.bfloat16)


def arrange(tensor, pair, padded):
    width = pair * padded
    slabs = round_up(width, LANES) // LANES
    return pl.pallas_call(
        functools.partial(arrange_kernel, pair, padded),
        out_shape=jax.ShapeDtypeStruct((2, width, width), tensor.dtype),
        scratch_shapes=[
            pltpu.VMEM((slabs, slabs * LANES, LANES), jnp.float32),
            pltpu.VMEM((slabs, slabs * LANES, LANES), jnp.float32),
            pltpu.VMEM((pair, padded, slabs * LANES), jnp.float32),
        ],
        name="arrange",
    )(tensor)


def sweep(rows, held, left, site, right, chi, pair, padded):
    chunk = CHUNK
    blocks = chi // chunk
    return pl.pallas_call(
        functools.partial(sweep_kernel, rows, chi, pair, padded, chunk),
        out_shape=jax.ShapeDtypeStruct((2,) + held.shape, held.dtype),
        in_specs=[pl.BlockSpec(memory_space=pltpu.VMEM)] * 4,
        out_specs=pl.BlockSpec(memory_space=pltpu.VMEM),
        scratch_shapes=[
            pltpu.VMEM((LANES, pair * LANES), jnp.bfloat16),
            pltpu.VMEM((chi * padded, LANES), jnp.float32),
            pltpu.VMEM((2, chi * padded, LANES), jnp.bfloat16),
            pltpu.VMEM((2, pair * LANES, LANES), jnp.bfloat16),
            pltpu.VMEM((pair * padded, chunk * LANES), jnp.bfloat16),
            pltpu.VMEM((chunk * padded, pair * LANES), jnp.bfloat16),
            pltpu.VMEM((chunk * padded, LANES), jnp.float32),
            pltpu.VMEM(held.shape, jnp.float32),
            pltpu.VMEM((8, LANES), jnp.float32),
            pltpu.VMEM((2,) + held.shape, jnp.bfloat16),
            pltpu.VMEM((2,) + held.shape, jnp.bfloat16),
            pltpu.VMEM((1, LANES), jnp.float32),
            pltpu.SemaphoreType.DMA((2, blocks)),
            pltpu.SemaphoreType.DMA((2, blocks)),
        ],
        compiler_params=pltpu.CompilerParams(collective_id=0, has_side_effects=True, vmem_limit_bytes=56 * 1024 * 1024),
        name="sweep",
    )(held, left, site, right)


def local(top_in, bottom_in, row_tensor, left_proj, right_proj):
    row_count = lax.axis_size("row")
    col_count = lax.axis_size("col")
    row_index = lax.axis_index("row")
    chi = top_in.shape[1]
    pair = row_tensor.shape[2]
    padded = round_up(pair, 8)

    ring = [(source, (source + 1) % col_count) for source in range(col_count)]
    left = lax.ppermute(left_proj[:, 0, 0], "col", ring)
    right = right_proj[:, 0, 0]
    sites = arrange(row_tensor[0, 0], pair, padded)

    held = jnp.where(row_index < row_count // 2, top_in[0], bottom_in[0])
    env = sweep(row_count, held, left, sites, right, chi, pair, padded)
    return env[:, None, None]


def solution(mesh):
    return jax.shard_map(
        local,
        mesh=mesh,
        in_specs=(
            P("col", None, None),
            P("col", None, None),
            P("row", "col", None, None, None),
            P(None, "row", "col", None, None),
            P(None, "row", "col", None, None),
        ),
        out_specs=P(None, "row", "col", None, None),
        check_vma=False,
    )
```
